128 devices in a mesh: dp: 16 (over z_lo, x, core), tensor: 8 (over y, z_hi).
Axes of the slice: x: 4, y: 4, z: 4 (z_hi: 2, z_lo: 2; z = z_hi * 2 + z_lo), core: 2. Of those that a mesh axis runs over, the one named last changes fastest.
Arguments:
- block_in: float32 [16384, 1024], P(('dp', 'tensor')), may hold values from -45 to 45
- norm1_gain: float32 [1024], replicated, may hold values from 0.25 to 1.75
- w_b: bfloat16 [1024, 1024], P('dp', 'tensor'), may hold values from -0.1875 to 0.1875
- w_c: bfloat16 [1024, 1024], P('dp', 'tensor'), may hold values from -0.1875 to 0.1875
- w_x: bfloat16 [1024, 1024], P('dp', 'tensor'), may hold values from -0.1875 to 0.1875
- conv_w: float32 [3, 1024], P(None, 'tensor'), may hold values from -3.5 to 3.5
- w_out: bfloat16 [1024, 1024], P('tensor', 'dp'), may hold values from -0.1875 to 0.1875
- norm2_gain: float32 [1024], replicated, may hold values from 0.25 to 1.75
- w_gate: bfloat16 [1024, 4608], P('dp', 'tensor'), may hold values from -0.1875 to 0.1875
- w_up: bfloat16 [1024, 4608], P('dp', 'tensor'), may hold values from -0.1875 to 0.1875
- w_down: bfloat16 [4608, 1024], P('tensor', 'dp'), may hold values from -0.09375 to 0.09375
- out_cot: float32 [16384, 1024], P(('dp', 'tensor')), may hold values from -6 to 6
Outputs:
- block_out: float32 [16384, 1024], P(('dp', 'tensor'))
- grad_in: float32 [16384, 1024], P(('dp', 'tensor'))
- grad_norm1: float32 [1024], replicated
- grad_w_b: float32 [1024, 1024], P('dp', 'tensor')
- grad_w_c: float32 [1024, 1024], P('dp', 'tensor')
- grad_w_x: float32 [1024, 1024], P('dp', 'tensor')
- grad_conv: float32 [3, 1024], P(None, 'tensor')
- grad_w_out: float32 [1024, 1024], P('tensor', 'dp')
- grad_norm2: float32 [1024], replicated
- grad_w_gate: float32 [1024, 4608], P('dp', 'tensor')
- grad_w_up: float32 [1024, 4608], P('dp', 'tensor')
- grad_w_down: float32 [4608, 1024], P('tensor', 'dp')
The draws below stay inside these ranges and needn't reach their ends.
All inputs are finite; a program needn't handle non-finite values.
Results may differ from the reference program's by a relative error of at most 0.022.
Values may be sent and summed in bfloat16 or wider, within the bound.
A program may use at most 64 MiB of HBM per device.

```python
import math
import jax
import jax.numpy as jnp
from jax import lax

D = 1024
FF = 4608
KW = 3
SEQ = 2048
TOKENS = 16384
OFFSET = 512


def draw_block_in(key, part):
    first, second, third = jax.random.split(key, 3)
    base = jnp.clip(jax.random.normal(first, (TOKENS, D), jnp.float32), -5.0, 5.0)
    rowscale = jnp.exp(jax.random.uniform(second, (TOKENS, 1), jnp.float32, 0.0, math.log(4.0)))
    colscale = jnp.exp(jax.random.uniform(third, (1, D), jnp.float32, math.log(0.5), math.log(2.0)))
    return base * rowscale * colscale


def shard_levels(key, extent, pieces, low, top_value):
    level = 1.0
    for axis_at, parts in pieces:
        draws = jax.random.uniform(jax.random.fold_in(jax.random.fold_in(key, 6), axis_at), (parts,), jnp.float32, low / len(pieces), top_value / len(pieces))
        level = level * jnp.repeat(jnp.exp(draws), extent[axis_at] // parts).reshape((-1,) + (1,) * (len(extent) - 1 - axis_at))
    return level


def normal_values(key, extent, scale, bound, cuts=(), held_as=jnp.bfloat16):
    entries = jax.random.normal(key, extent, jnp.float32) * scale
    if len(cuts) > 0:
        entries = shard_levels(key, extent, cuts, -0.22, 0.18) * entries
    return jnp.clip(entries, min=-bound, max=bound).astype(held_as)


def setup_inputs(seed: int = 0) -> dict:
    keys = jax.random.split(jax.random.key(seed), 13)
    return {
        "block_in": draw_block_in(jax.random.fold_in(keys[12], 71), 0),
        "norm1_gain": jnp.clip(1.0 + 0.15 * jax.random.normal(keys[1], (D,), jnp.float32), 0.25, 1.75),
        "w_b": normal_values(keys[2], (D, D), D ** -0.5, 0.1875, ((0, 16), (1, 8))),
        "w_c": normal_values(keys[3], (D, D), D ** -0.5, 0.1875, ((0, 16), (1, 8))),
        "w_x": normal_values(keys[4], (D, D), D ** -0.5, 0.1875, ((0, 16), (1, 8))),
        "conv_w": normal_values(keys[5], (KW, D), KW ** -0.5, 3.5, ((1, 8),), jnp.float32),
        "w_out": normal_values(keys[6], (D, D), D ** -0.5, 0.1875, ((0, 8), (1, 16))),
        "norm2_gain": jnp.clip(1.0 + 0.15 * jax.random.normal(keys[7], (D,), jnp.float32), 0.25, 1.75),
        "w_gate": normal_values(keys[8], (D, FF), D ** -0.5, 0.1875, ((0, 16), (1, 8))),
        "w_up": normal_values(keys[9], (D, FF), D ** -0.5, 0.1875, ((0, 16), (1, 8))),
        "w_down": normal_values(keys[10], (FF, D), FF ** -0.5, 0.09375, ((0, 8), (1, 16))),
        "out_cot": normal_values(keys[11], (TOKENS, D), 1.0, 6.0, ((0, 128),), jnp.float32),
    }


EPS = 1e-06

def tdot(left, right):
    return lax.dot_general(left, right, (((0,), (0,)), ((), ())), preferred_element_type=jnp.float32)

def ndot(left, right):
    return lax.dot_general(left, right, (((1,), (1,)), ((), ())), preferred_element_type=jnp.float32)

def one_sequence(xin, cot, cutoff, norm1_gain, w_b, w_c, w_x, conv_w, w_out, norm2_gain, w_gate, w_up, w_down):
    length = xin.shape[0]
    rows = jnp.arange(length, dtype=jnp.int32)[:, None]
    segment = rows >= cutoff
    mask_one = jnp.where((rows >= 1) & ((rows - 1 >= cutoff) == segment), 1.0, 0.0).astype(jnp.float32)
    mask_two = jnp.where((rows >= 2) & ((rows - 2 >= cutoff) == segment), 1.0, 0.0).astype(jnp.float32)
    r1 = lax.rsqrt(lax.optimization_barrier(jnp.mean(xin * xin, -1, keepdims=True)) + EPS)
    n1 = xin * r1
    h1 = (n1 * norm1_gain).astype(jnp.bfloat16)
    bproj = jnp.dot(h1, w_b, preferred_element_type=jnp.float32)
    cproj = jnp.dot(h1, w_c, preferred_element_type=jnp.float32)
    xproj = jnp.dot(h1, w_x, preferred_element_type=jnp.float32)
    gated = bproj * xproj
    extended = jnp.concatenate([jnp.zeros((2, D), jnp.float32), gated], 0)
    conv = conv_w[0] * extended[:-2] * mask_two + conv_w[1] * extended[1:-1] * mask_one + conv_w[2] * gated
    ymix = (cproj * conv).astype(jnp.bfloat16)
    mid = xin + jnp.dot(ymix, w_out, preferred_element_type=jnp.float32)
    r2 = lax.rsqrt(lax.optimization_barrier(jnp.mean(mid * mid, -1, keepdims=True)) + EPS)
    n2 = mid * r2
    h2 = (n2 * norm2_gain).astype(jnp.bfloat16)
    gate = jnp.dot(h2, w_gate, preferred_element_type=jnp.float32)
    up = jnp.dot(h2, w_up, preferred_element_type=jnp.float32)
    sig = jax.nn.sigmoid(gate)
    act = (gate * sig * up).astype(jnp.bfloat16)
    block_out = mid + jnp.dot(act, w_down, preferred_element_type=jnp.float32)
    cot_b = cot.astype(jnp.bfloat16)
    g_down = tdot(act, cot_b)
    dact = ndot(cot_b, w_down)
    dgate = (dact * up * sig * (1.0 + gate * (1.0 - sig))).astype(jnp.bfloat16)
    dup = (dact * gate * sig).astype(jnp.bfloat16)
    g_gate = tdot(h2, dgate)
    g_up = tdot(h2, dup)
    dh2 = ndot(dgate, w_gate) + ndot(dup, w_up)
    g_n2 = lax.optimization_barrier(jnp.sum(dh2 * n2, 0))
    dn2 = dh2 * norm2_gain
    dmid = cot + r2 * (dn2 - n2 * lax.optimization_barrier(jnp.mean(dn2 * n2, -1, keepdims=True)))
    dmid_b = dmid.astype(jnp.bfloat16)
    g_out = tdot(ymix, dmid_b)
    dy = ndot(dmid_b, w_out)
    dc = (dy * conv).astype(jnp.bfloat16)
    dconv = dy * cproj
    masked_one = dconv * mask_one
    masked_two = dconv * mask_two
    zeros_two = jnp.zeros((2, D), jnp.float32)
    next_one = jnp.concatenate([masked_one[1:], zeros_two[:1]], 0)
    next_two = jnp.concatenate([masked_two[2:], zeros_two], 0)
    dgated = conv_w[2] * dconv + conv_w[1] * next_one + conv_w[0] * next_two
    g_conv = jnp.stack([lax.optimization_barrier(jnp.sum(dconv * extended[:-2] * mask_two, 0)), lax.optimization_barrier(jnp.sum(dconv * extended[1:-1] * mask_one, 0)), lax.optimization_barrier(jnp.sum(dconv * gated, 0))], 0)
    db = (dgated * xproj).astype(jnp.bfloat16)
    dx = (dgated * bproj).astype(jnp.bfloat16)
    g_b = tdot(h1, db)
    g_c = tdot(h1, dc)
    g_x = tdot(h1, dx)
    dh1 = ndot(db, w_b) + ndot(dc, w_c) + ndot(dx, w_x)
    g_n1 = lax.optimization_barrier(jnp.sum(dh1 * n1, 0))
    dn1 = dh1 * norm1_gain
    grad_in = dmid + r1 * (dn1 - n1 * lax.optimization_barrier(jnp.mean(dn1 * n1, -1, keepdims=True)))
    return (block_out, grad_in, (g_n1, g_b, g_c, g_x, g_conv, g_out, g_n2, g_gate, g_up, g_down))

def reference(block_in, norm1_gain, w_b, w_c, w_x, conv_w, w_out, norm2_gain, w_gate, w_up, w_down, out_cot):
    count = TOKENS // SEQ
    rolled_in = jnp.roll(block_in, -OFFSET, axis=0)
    rolled_cot = jnp.roll(out_cot, -OFFSET, axis=0)
    cutoffs = jnp.where(jnp.arange(count, dtype=jnp.int32) == count - 1, jnp.int32(SEQ - OFFSET), jnp.int32(SEQ)).astype(jnp.int32)
    inputs = (rolled_in.reshape(count, SEQ, D), rolled_cot.reshape(count, SEQ, D), cutoffs)
    start = (jnp.zeros((D,), jnp.float32), jnp.zeros((D, D), jnp.float32), jnp.zeros((D, D), jnp.float32), jnp.zeros((D, D), jnp.float32), jnp.zeros((3, D), jnp.float32), jnp.zeros((D, D), jnp.float32), jnp.zeros((D,), jnp.float32), jnp.zeros((D, FF), jnp.float32), jnp.zeros((D, FF), jnp.float32), jnp.zeros((FF, D), jnp.float32))

    def step_fn(carry, item):
        outs, grads, terms = one_sequence(item[0], item[1], item[2], norm1_gain, w_b, w_c, w_x, conv_w, w_out, norm2_gain, w_gate, w_up, w_down)
        return (tuple((a + b for a, b in zip(carry, terms))), (outs, grads))
    totals, stacked = lax.scan(step_fn, start, inputs)
    block_out = jnp.roll(stacked[0].reshape(TOKENS, D), OFFSET, axis=0)
    grad_in = jnp.roll(stacked[1].reshape(TOKENS, D), OFFSET, axis=0)
    return (block_out, grad_in, totals[0], totals[1], totals[2], totals[3], totals[4], totals[5], totals[6], totals[7], totals[8], totals[9])
```

```python
import functools

import jax
import jax.numpy as jnp
from jax import lax
from jax.experimental import pallas as pl
from jax.experimental.pallas import tpu as pltpu
from jax.sharding import PartitionSpec as P

SEQ = 2048
OFFSET = 512
EPS = 1e-06
BF = jnp.bfloat16
F32 = jnp.float32
MESH = pl.DeviceIdType.MESH
RING = 4
VMEM_LIMIT = 60 * 1024 * 1024


def tdot(left, right):
    return lax.dot_general(
        left, right, (((0,), (0,)), ((), ())), preferred_element_type=F32
    )


def ndot(left, right):
    return lax.dot_general(
        left, right, (((1,), (1,)), ((), ())), preferred_element_type=F32
    )


def dot(left, right):
    return jnp.dot(left, right, preferred_element_type=F32)


class Place:
    def __init__(self):
        dp, t = lax.axis_index("dp"), lax.axis_index("tensor")
        self.c, self.x = lax.rem(dp, 2), lax.rem(lax.div(dp, 2), RING)
        self.y, self.zhi = lax.div(t, 2), lax.rem(t, 2)
        self.z = self.zhi * 2 + lax.div(dp, 8)

    def at(self, x=None, y=None, z=None, c=None):
        x = self.x if x is None else x
        y = self.y if y is None else y
        z = self.z if z is None else z
        c = self.c if c is None else c
        return (lax.rem(z, 2) * 8 + x * 2 + c, y * 2 + lax.div(z, 2))

    def ring(self, axis):
        p = getattr(self, axis)
        ids = [self.at(**{axis: lax.rem(p + d, RING)}) for d in (1, 3, 2)]
        return (p, *ids)

    def partner(self):
        return self.at(c=1 - self.c)


class Links:
    def __init__(self, send, recv, local=None):
        self.send, self.recv, self.local = send, recv, local
        self.n = 0
        self.m = 0
        self.sent = []

    def push(self, src, dst, dev):
        copy = pltpu.make_async_remote_copy(
            src_ref=src, dst_ref=dst, send_sem=self.send.at[self.n],
            recv_sem=self.recv.at[self.n], device_id=dev, device_id_type=MESH,
        )
        self.n += 1
        copy.start()
        self.sent.append(copy)
        return copy

    def near(self, src, dst):
        copy = pltpu.make_async_copy(src, dst, self.local.at[self.m])
        self.m += 1
        copy.start()
        return copy

    def close(self):
        for copy in self.sent:
            copy.wait_send()


def greet(devs):
    barrier = pltpu.get_barrier_semaphore()
    for dev in devs:
        pl.semaphore_signal(barrier, inc=1, device_id=dev, device_id_type=MESH)
    pl.semaphore_wait(barrier, len(devs))


def ring_gather(links, ring, slot, own=None, arrived=None):
    p, right, left, _ = ring
    own = own or (lambda h: slot(p, h))
    arrived = arrived or (lambda k, h: None)
    r0 = links.push(own(0), slot(p, 0), right)
    l1 = links.push(own(1), slot(p, 1), left)
    r1 = links.push(own(1), slot(p, 1), right)
    l0 = links.push(own(0), slot(p, 0), left)
    before, after, far = lax.rem(p + 3, RING), lax.rem(p + 1, RING), lax.rem(p + 2, RING)
    yield
    r0.wait_recv()
    f0 = links.push(slot(before, 0), slot(before, 0), right)
    arrived(before, 0)
    l1.wait_recv()
    f1 = links.push(slot(after, 1), slot(after, 1), left)
    arrived(after, 1)
    yield
    r1.wait_recv()
    arrived(before, 1)
    l0.wait_recv()
    arrived(after, 0)
    f0.wait_recv()
    arrived(far, 0)
    f1.wait_recv()
    arrived(far, 1)


def ring_reduce(links, ring, part, buf, add, finish):
    p, right, left, _ = ring
    before, after, far = lax.rem(p + 3, RING), lax.rem(p + 1, RING), lax.rem(p + 2, RING)
    a = links.push(part(far, 0), buf[0], right)
    b = links.push(part(far, 1), buf[1], left)
    c = links.push(part(after, 1), buf[2], right)
    d = links.push(part(before, 0), buf[3], left)
    yield
    a.wait_recv()
    add(buf[0], part(after, 0))
    f = links.push(buf[0], buf[4], right)
    b.wait_recv()
    add(buf[1], part(before, 1))
    g = links.push(buf[1], buf[5], left)
    yield
    d.wait_recv()
    f.wait_recv()
    finish(0, part(p, 0), buf[3], buf[4])
    c.wait_recv()
    g.wait_recv()
    finish(1, part(p, 1), buf[2], buf[5])


def drain(gen):
    for _ in gen:
        pass


def rows_of(q):
    return pl.ds(16 * q, 16)


def weight_gather(links, at, full):
    x, z, c = at.x, at.z, at.c
    ring_x, ring_z, mate = at.ring("x"), at.ring("z"), at.partner()
    a1 = ring_gather(links, ring_z, lambda k, h: full.at[:, k, x, c, rows_of(h)])
    b1 = ring_gather(links, ring_x, lambda k, h: full.at[:, z, k, c, rows_of(2 + h)])
    for _ in range(3):
        next(a1, None)
        next(b1, None)
        yield

    crossed = []

    def cross(view):
        crossed.append(links.push(view, view, mate))

    slot_a = lambda k, h: full.at[:, :, k, c, rows_of(h)]
    slot_b = lambda k, h: full.at[:, k, :, c, rows_of(2 + h)]
    a2 = ring_gather(links, ring_x, slot_a, arrived=lambda k, h: cross(slot_a(k, h)))
    b2 = ring_gather(links, ring_z, slot_b, arrived=lambda k, h: cross(slot_b(k, h)))
    next(a2)
    next(b2)
    for h in range(2):
        cross(slot_a(x, h))
        cross(slot_b(z, h))
    yield
    for _ in range(2):
        next(a2, None)
        next(b2, None)
        yield
    for copy in crossed:
        copy.wait_recv()


def add_rows(dst, src):
    if len(dst.shape) == 3:
        for i in range(dst.shape[0]):
            dst[i] = (dst[i].astype(F32) + src[i].astype(F32)).astype(dst.dtype)
        return

    def body(i, _):
        l, k = lax.div(i, RING), lax.rem(i, RING)
        dst[l, k] = (dst[l, k].astype(F32) + src[l, k].astype(F32)).astype(dst.dtype)
        return 0

    lax.fori_loop(0, dst.shape[0] * RING, body, 0)


def weight_reduce(links, at, grads, landed, total, bufs1, bufs2, out):
    x, z, c = at.x, at.z, at.c
    ring_x, ring_z, mate = at.ring("x"), at.ring("z"), at.partner()
    arrays = grads.shape[0]
    swaps = [
        links.push(grads.at[:, k, :, 1 - c], landed.at[:, k], mate) for k in range(RING)
    ]
    yield
    for k in range(RING):
        swaps[k].wait_recv()

        def body(i, _, k=k):
            l, j = lax.div(i, RING), lax.rem(i, RING)
            both = grads[l, k, j, c].astype(F32) + landed[l, k, j].astype(F32)
            total[l, k, j] = both.astype(BF)
            return 0

        lax.fori_loop(0, arrays * RING, body, 0)
    yield

    def finish1(view):
        def run(h, own, one, two):
            def body(i, _):
                l, k = lax.div(i, RING), lax.rem(i, RING)
                s = own[l, k].astype(F32) + one[l, k].astype(F32) + two[l, k].astype(F32)
                own[l, k] = s.astype(BF)
                return 0

            lax.fori_loop(0, arrays * RING, body, 0)

        return run

    part_a = lambda k, h: total.at[:, :, k, rows_of(h)]
    part_b = lambda k, h: total.at[:, k, :, rows_of(2 + h)]
    a1 = ring_reduce(links, ring_x, part_a, [bufs1.at[0, i] for i in range(6)], add_rows, finish1(0))
    b1 = ring_reduce(links, ring_z, part_b, [bufs1.at[1, i] for i in range(6)], add_rows, finish1(1))
    for _ in range(3):
        next(a1, None)
        next(b1, None)
        yield

    def finish2(color):
        def run(h, own, one, two):
            for l in range(arrays):
                s = own[l].astype(F32) + one[l].astype(F32) + two[l].astype(F32)
                out[l, rows_of(2 * color + h)] = s

        return run

    part_a2 = lambda k, h: total.at[:, k, x, rows_of(h)]
    part_b2 = lambda k, h: total.at[:, z, k, rows_of(2 + h)]
    a2 = ring_reduce(links, ring_z, part_a2, [bufs2.at[0, i] for i in range(6)], add_rows, finish2(0))
    b2 = ring_reduce(links, ring_x, part_b2, [bufs2.at[1, i] for i in range(6)], add_rows, finish2(1))
    for _ in range(3):
        next(a2, None)
        next(b2, None)
        yield


def half(ref, k, h):
    return ref.at[k, pl.ds(64 * h, 64)]


def add_tokens(dst, src):
    for i in range(4):
        r = rows_of(i)
        dst[r] = (dst[r].astype(F32) + src[r].astype(F32)).astype(BF)


def call(body, out_shape, out_specs, in_specs, scratch, cid, args):
    return pl.pallas_call(
        body,
        out_shape=out_shape,
        in_specs=in_specs,
        out_specs=out_specs,
        scratch_shapes=scratch,
        compiler_params=pltpu.CompilerParams(
            collective_id=cid, has_side_effects=True, vmem_limit_bytes=VMEM_LIMIT
        ),
    )(*args)


VM = pl.BlockSpec(memory_space=pltpu.VMEM)
ANY = pl.BlockSpec(memory_space=pl.ANY)


def sds(shape, dtype):
    return jax.ShapeDtypeStruct(shape, dtype)


def sems(n):
    return pltpu.SemaphoreType.DMA((n,))


def enter_kernel(
    x_ref, gain_ref, wb, wc, wx, wo, taps_ref,
    h_ref, ob, oc, ox, oo, taps_out,
    full, send, recv, local,
):
    at = Place()
    links = Links(send, recv, local)
    ring_y, ring_x, ring_z = at.ring("y"), at.ring("x"), at.ring("z")
    own = [links.near(w, full.at[i, at.z, at.x, at.c]) for i, w in enumerate((wb, wc, wx, wo))]
    p = at.y
    for i in range(8):
        r = rows_of(i)
        v = x_ref[r]
        r1 = lax.rsqrt(jnp.mean(v * v, -1, keepdims=True) + EPS)
        h_ref[p, r] = (v * r1 * gain_ref[...]).astype(BF)
    taps_out[at.zhi] = taps_ref[...]
    far_z = ring_z[3]
    greet([*ring_y[1:3], *ring_x[1:3], *ring_z[1:4], at.partner()])
    tokens = ring_gather(links, ring_y, lambda k, h: half(h_ref, k, h))
    next(tokens)
    for copy in own:
        copy.wait()
    weights = weight_gather(links, at, full)
    next(weights)
    tap = links.push(taps_ref, taps_out.at[at.zhi], far_z)
    next(weights)
    next(tokens)
    drain(weights)
    outs = []
    for i, o in enumerate((ob, oc, ox, oo)):
        for s in range(2):
            outs.append(
                links.near(full.at[i, pl.ds(2 * s, 2)], o.at[:, :, :, :, pl.ds(128 * s, 128)])
            )
    drain(tokens)
    tap.wait_recv()
    for copy in outs:
        copy.wait()
    links.close()


def enter(block_in, gain, wb, wc, wx, wo, taps):
    w = sds((2, 4, 2, 64, 256), BF)
    return call(
        enter_kernel,
        [sds((RING, 128, 1024), BF), w, w, w, w, sds((2, 3, 128), F32)],
        [VM, ANY, ANY, ANY, ANY, VM],
        [VM, VM, ANY, ANY, ANY, ANY, VM],
        [pltpu.VMEM((4, 4, 4, 2, 64, 128), BF), sems(64), sems(64), sems(16)],
        0,
        (block_in, gain, wb, wc, wx, wo, taps),
    )


def middle_kernel(
    part_ref, x_ref, gain_ref, cot_ref, wg, wu, wd,
    mid_ref, h_ref, cots_ref, g0, g1, u0, u1, d0, d1,
    full, land, send, recv, local,
):
    at = Place()
    links = Links(send, recv, local)
    ring_y, ring_x, ring_z = at.ring("y"), at.ring("x"), at.ring("z")
    own = [links.near(w, full.at[i, at.z, at.x, at.c]) for i, w in enumerate((wg, wu, wd))]
    p = at.y
    greet([*ring_y[1:3], *ring_x[1:3], *ring_z[1:3], at.partner()])

    def finish(h, mine, one, two):
        for i in range(4):
            r = rows_of(i)
            g = pl.ds(64 * h + 16 * i, 16)
            s = mine[r].astype(F32) + one[r].astype(F32) + two[r].astype(F32)
            v = x_ref[g] + s
            mid_ref[g] = v
            r2 = lax.rsqrt(jnp.mean(v * v, -1, keepdims=True) + EPS)
            h_ref[p, g] = (v * r2 * gain_ref[...]).astype(BF)

    reduce = ring_reduce(
        links, ring_y, lambda k, h: half(part_ref, k, h),
        [land.at[i] for i in range(6)], add_tokens, finish,
    )
    next(reduce)
    for copy in own:
        copy.wait()
    weights = weight_gather(links, at, full)
    next(weights)
    for i in range(8):
        r = rows_of(i)
        cots_ref[p, r] = cot_ref[r].astype(BF)
    next(reduce)
    next(weights)
    next(weights)
    next(reduce, None)
    tokens = ring_gather(links, ring_y, lambda k, h: half(h_ref, k, h))
    next(tokens)
    next(weights)
    cots = ring_gather(links, ring_y, lambda k, h: half(cots_ref, k, h))
    next(tokens)
    next(cots)
    next(weights)
    next(cots)
    drain(tokens)
    drain(weights)
    outs = []
    for i, pair in enumerate(((g0, g1), (u0, u1), (d0, d1))):
        for s in range(2):
            outs.append(links.near(full.at[i, pl.ds(2 * s, 2)], pair[s]))
    drain(cots)
    for copy in outs:
        copy.wait()
    links.close()


def middle(part, block_in, gain, cot, wg, wu, wd):
    w = sds((2, 4, 2, 64, 576), BF)
    tokens = sds((RING, 128, 1024), BF)
    return call(
        middle_kernel,
        [sds((128, 1024), F32), tokens, tokens] + [w] * 6,
        [VM, VM, VM] + [ANY] * 6,
        [VM, VM, VM, VM, ANY, ANY, ANY],
        [
            pltpu.VMEM((3, 4, 4, 2, 64, 576), BF), pltpu.VMEM((6, 64, 1024), BF),
            sems(80), sems(80), sems(16),
        ],
        1,
        (part, block_in, gain, cot, wg, wu, wd),
    )


def turn_kernel(
    down_ref, back_ref, mid_ref, gain_ref, cot_ref, g0, g1, u0, u1, d0, d1,
    out_ref, dmid_ref, dmids_ref, norm_ref, grad_ref,
    grads, landed, total, bufs1, bufs2, land, send, recv, local,
):
    at = Place()
    links = Links(send, recv, local)
    ring_y, ring_x, ring_z = at.ring("y"), at.ring("x"), at.ring("z")
    own = []
    for i, pair in enumerate(((g0, g1), (u0, u1), (d0, d1))):
        for s in range(2):
            own.append(links.near(pair[s], grads.at[i, pl.ds(2 * s, 2)]))
    p = at.y
    norm_ref[...] = jnp.zeros_like(norm_ref)
    greet([*ring_y[1:3], *ring_x[1:3], *ring_z[1:3], at.partner()])

    def finish(h, mine, one, two):
        for i in range(4):
            r = rows_of(i)
            g = pl.ds(64 * h + 16 * i, 16)
            dh = mine[r].astype(F32) + one[r].astype(F32) + two[r].astype(F32)
            v = mid_ref[g]
            r2 = lax.rsqrt(jnp.mean(v * v, -1, keepdims=True) + EPS)
            n2 = v * r2
            t = dh * n2
            norm_ref[...] += t[:8] + t[8:]
            dn = dh * gain_ref[...]
            dm = cot_ref[g] + r2 * (dn - n2 * jnp.mean(dn * n2, -1, keepdims=True))
            dmid_ref[g] = dm
            dmids_ref[p, g] = dm.astype(BF)

    def finish_out(h, mine, one, two):
        for i in range(4):
            r = rows_of(i)
            g = pl.ds(64 * h + 16 * i, 16)
            s = mine[r].astype(F32) + one[r].astype(F32) + two[r].astype(F32)
            out_ref[g] = mid_ref[g] + s

    back = ring_reduce(
        links, ring_y, lambda k, h: half(back_ref, k, h),
        [land.at[0, i] for i in range(6)], add_tokens, finish,
    )
    next(back)
    for copy in own:
        copy.wait()
    weights = weight_reduce(links, at, grads, landed, total, bufs1, bufs2, grad_ref)
    next(weights)
    next(back)
    next(weights)
    next(weights)
    next(back, None)
    tokens = ring_gather(links, ring_y, lambda k, h: half(dmids_ref, k, h))
    next(tokens)
    outs = ring_reduce(
        links, ring_y, lambda k, h: half(down_ref, k, h),
        [land.at[1, i] for i in range(6)], add_tokens, finish_out,
    )
    next(weights)
    next(tokens)
    next(outs)
    next(weights)
    next(weights)
    next(outs)
    next(weights)
    drain(tokens)
    drain(outs)
    drain(weights)
    links.close()


def turn(down, back, mid, gain, cot, grads):
    row = sds((128, 1024), F32)
    return call(
        turn_kernel,
        [row, row, sds((RING, 128, 1024), BF), sds((8, 1024), F32), sds((3, 64, 576), F32)],
        [VM] * 5,
        [VM] * 5 + [ANY] * 6,
        [
            pltpu.VMEM((3, 4, 4, 2, 64, 576), BF), pltpu.VMEM((3, 4, 4, 64, 576), BF),
            pltpu.VMEM((3, 4, 4, 64, 576), BF), pltpu.VMEM((2, 6, 3, 4, 16, 576), BF),
            pltpu.VMEM((2, 6, 3, 16, 576), BF), pltpu.VMEM((2, 6, 64, 1024), BF),
            sems(64), sems(64), sems(16),
        ],
        2,
        (down, back, mid, gain, cot, *grads),
    )


def leave_kernel(
    part_ref, x_ref, gain_ref, dmid_ref, small_ref, gb, gc, gx, go,
    gin_ref, grad_ref, sum_ref,
    grads, landed, total, bufs1, bufs2, land, small, send, recv, local,
):
    at = Place()
    links = Links(send, recv, local)
    ring_y, ring_x, ring_z = at.ring("y"), at.ring("x"), at.ring("z")
    own = []
    for i, g in enumerate((gb, gc, gx, go)):
        for s in range(2):
            own.append(
                links.near(g.at[:, :, :, :, pl.ds(128 * s, 128)], grads.at[i, pl.ds(2 * s, 2)])
            )
    greet([*ring_y[1:4], *ring_x[1:4], *ring_z[1:4], at.partner()])
    norm = [jnp.zeros((8, 1024), F32)]

    def finish(h, mine, one, two):
        for i in range(4):
            r = rows_of(i)
            g = pl.ds(64 * h + 16 * i, 16)
            dh = mine[r].astype(F32) + one[r].astype(F32) + two[r].astype(F32)
            v = x_ref[g]
            r1 = lax.rsqrt(jnp.mean(v * v, -1, keepdims=True) + EPS)
            n1 = v * r1
            t = dh * n1
            norm[0] = norm[0] + t[:8] + t[8:]
            dn = dh * gain_ref[...]
            gin_ref[g] = dmid_ref[g] + r1 * (dn - n1 * jnp.mean(dn * n1, -1, keepdims=True))

    back = ring_reduce(
        links, ring_y, lambda k, h: half(part_ref, k, h),
        [land.at[i] for i in range(6)], add_tokens, finish,
    )
    next(back)
    for copy in own:
        copy.wait()
    weights = weight_reduce(links, at, grads, landed, total, bufs1, bufs2, grad_ref)
    next(weights)
    next(back)
    next(weights)
    next(weights)
    next(back, None)
    first = lax.broadcasted_iota(jnp.int32, (8, 1024), 0) == 0
    total_norm = jnp.sum(norm[0], 0, keepdims=True)
    value = small_ref[...] + jnp.where(first, total_norm, 0.0)
    stages = (("y", ring_y), ("x", ring_x), ("z", ring_z))
    for s, (axis, ring) in enumerate(stages):
        pos = ring[0]
        small[s, pos] = value
        copies = [links.push(small.at[s, pos], small.at[s, pos], dev) for dev in ring[1:4]]
        next(weights, None)
        for copy in copies:
            copy.wait_recv()
        value = (small[s, 0] + small[s, 1]) + (small[s, 2] + small[s, 3])
    small[3, at.c] = value
    copy = links.push(small.at[3, at.c], small.at[3, at.c], at.partner())
    next(weights, None)
    copy.wait_recv()
    sum_ref[...] = small[3, 0] + small[3, 1]
    drain(weights)
    links.close()


def leave(part, block_in, gain, dmid, small, grads):
    return call(
        leave_kernel,
        [sds((128, 1024), F32), sds((4, 64, 128), F32), sds((8, 1024), F32)],
        [VM] * 3,
        [VM] * 5 + [ANY] * 4,
        [
            pltpu.VMEM((4, 4, 4, 2, 64, 128), BF), pltpu.VMEM((4, 4, 4, 64, 128), BF),
            pltpu.VMEM((4, 4, 4, 64, 128), BF), pltpu.VMEM((2, 6, 4, 4, 16, 128), BF),
            pltpu.VMEM((2, 6, 4, 16, 128), BF), pltpu.VMEM((6, 64, 1024), BF),
            pltpu.VMEM((4, 4, 8, 1024), F32), sems(64), sems(64), sems(16),
        ],
        3,
        (part, block_in, gain, dmid, small, *grads),
    )


def halo_routes(n_dp, step):
    swap = [(d * 8 + t, d * 8 + (t ^ 1)) for d in range(n_dp) for t in range(8)]
    if step > 0:
        cross = [(d * 8 + t, d * 8 + 8 + t - 1) for d in range(n_dp - 1) for t in (1, 3, 5, 7)]
    else:
        cross = [(d * 8 + t, d * 8 - 8 + t + 1) for d in range(1, n_dp) for t in (0, 2, 4, 6)]
    return swap, cross


def per_device(
    block_in, norm1_gain, w_b, w_c, w_x, conv_w, w_out, norm2_gain, w_gate, w_up, w_down, out_cot
):
    axes = ("dp", "tensor")
    dp, t = lax.axis_index("dp"), lax.axis_index("tensor")
    n_dp = lax.axis_size("dp")
    zhi = t % 2
    gain1, gain2 = norm1_gain[None, :], norm2_gain[None, :]
    h1, wb, wc, wx, wo, taps = enter(block_in, gain1, w_b, w_c, w_x, w_out.T, conv_w)
    wb, wc, wx, wo = (w.reshape(1024, 256) for w in (wb, wc, wx, wo))
    taps = taps.transpose(1, 0, 2).reshape(3, 256)
    h1 = h1.reshape(512, 1024)
    block = dp * 8 + 2 * jnp.arange(RING, dtype=jnp.int32) + zhi
    begins = lambda r: (r == 0) | ((r * 128 + SEQ - OFFSET) % SEQ == 0)
    keep_back = jnp.where(begins(block), 0.0, 1.0).astype(F32)[:, None, None]
    following = block + 1
    keep_fwd = jnp.where(
        begins(following) | (following == n_dp * 8), 0.0, 1.0
    ).astype(F32)[:, None, None]

    bproj, xproj = dot(h1, wb), dot(h1, wx)
    gated = (bproj * xproj).reshape(RING, 128, 256)
    swap, cross = halo_routes(n_dp, 1)
    tails = gated[:, -2:]
    near = lax.ppermute(tails, axes, swap)
    wrap = lax.ppermute(tails[-1:], axes, cross)
    cproj = dot(h1, wc).reshape(RING, 128, 256)
    shifted = jnp.concatenate([wrap, near[:-1]], 0)
    halo = jnp.where(zhi == 1, near, shifted) * keep_back
    extended = jnp.concatenate([halo, gated], 1)
    two, one = extended[:, :-2], extended[:, 1:-1]
    conv = taps[0] * two + taps[1] * one + taps[2] * gated
    ymix = (cproj * conv).astype(BF).reshape(512, 256)
    part = ndot(ymix, wo).astype(BF).reshape(RING, 128, 1024)
    mid, h2, cots, *ffn = middle(part, block_in, gain2, out_cot, w_gate, w_up, w_down.T)
    wg, wu, wd = ([w.reshape(1024, 576) for w in ffn[2 * i : 2 * i + 2]] for i in range(3))
    h2, cots = h2.reshape(512, 1024), cots.reshape(512, 1024)
    down, back = 0.0, 0.0
    g_gate, g_up, g_down = [], [], []
    for s in range(2):
        gate, up = dot(h2, wg[s]), dot(h2, wu[s])
        sig = jax.nn.sigmoid(gate)
        act = (gate * sig * up).astype(BF)
        dact = dot(cots, wd[s])
        dgate = (dact * up * sig * (1.0 + gate * (1.0 - sig))).astype(BF)
        dup = (dact * gate * sig).astype(BF)
        down = down + ndot(act, wd[s])
        back = back + ndot(dgate, wg[s]) + ndot(dup, wu[s])
        split = lambda g: g.astype(BF).reshape(2, 4, 2, 64, 576)
        g_gate.append(split(tdot(h2, dgate)))
        g_up.append(split(tdot(h2, dup)))
        g_down.append(split(tdot(cots, act)))
    tokens = lambda v: v.astype(BF).reshape(RING, 128, 1024)
    block_out, dmid, dmids, sums2, ffn_grads = turn(
        tokens(down), tokens(back), mid, gain2, out_cot, (*g_gate, *g_up, *g_down)
    )
    dmids = dmids.reshape(512, 1024)
    dy = dot(dmids, wo)
    dy = dy.reshape(RING, 128, 256)
    dconv = dy * cproj
    swap, cross = halo_routes(n_dp, -1)
    heads = dconv[:, :2]
    near = lax.ppermute(heads, axes, swap)
    wrap = lax.ppermute(heads[:1], axes, cross)
    g_out = tdot(dmids, ymix)
    dc = (dy * conv).astype(BF).reshape(512, 256)
    shifted = jnp.concatenate([near[1:], wrap], 0)
    halo = jnp.where(zhi == 0, near, shifted) * keep_fwd
    after = jnp.concatenate([dconv, halo], 1)
    dgated = taps[2] * dconv + taps[1] * after[:, 1:-1] + taps[0] * after[:, 2:]
    dgated = dgated.reshape(512, 256)
    part_conv = jnp.stack(
        [jnp.sum(dconv * v, (0, 1)) for v in (two, one, gated)], 0
    )
    db = (dgated * xproj).astype(BF)
    dx = (dgated * bproj).astype(BF)
    part1 = tokens(ndot(db, wb) + ndot(dc, wc) + ndot(dx, wx))
    split = lambda g: g.astype(BF).reshape(2, 4, 2, 64, 256)
    small = jnp.zeros((8, 1024), F32)
    small = small.at[1].set(jnp.sum(sums2, 0))
    small = lax.dynamic_update_slice(small, part_conv, (jnp.int32(2), (t // 2) * 256))
    grad_in, mix_grads, total = leave(
        part1, block_in, gain1, dmid, small,
        (split(tdot(h1, db)), split(tdot(h1, dc)), split(tdot(h1, dx)), split(g_out)),
    )
    grad_conv = lax.dynamic_slice(total, (jnp.int32(2), t * 128), (3, 128))
    return (
        block_out, grad_in, total[0], mix_grads[0], mix_grads[1], mix_grads[2], grad_conv,
        mix_grads[3].T, total[1], ffn_grads[0], ffn_grads[1], ffn_grads[2].T,
    )


def solution(mesh):
    tok, mat, tam = P(("dp", "tensor"), None), P("dp", "tensor"), P("tensor", "dp")
    taps = P(None, "tensor")
    return jax.shard_map(
        per_device,
        mesh=mesh,
        in_specs=(tok, P(), mat, mat, mat, taps, tam, P(), mat, mat, tam, tok),
        out_specs=(tok, tok, P(), mat, mat, mat, taps, tam, P(), mat, mat, tam),
        check_vma=False,
    )
```

```python
import jax
import jax.numpy as jnp
from jax import lax
from jax.experimental import pallas as pl
from jax.experimental.pallas import tpu as pltpu
from jax.sharding import PartitionSpec as P

SEQ = 2048
OFFSET = 512
EPS = 1e-06
BF = jnp.bfloat16
F32 = jnp.float32
MESH = pl.DeviceIdType.MESH
RING = 4
VMEM_LIMIT = 63 * 1024 * 1024


def tdot(left, right):
    return lax.dot_general(
        left, right, (((0,), (0,)), ((), ())), preferred_element_type=F32
    )


def ndot(left, right):
    return lax.dot_general(
        left, right, (((1,), (1,)), ((), ())), preferred_element_type=F32
    )


def dot(left, right):
    return jnp.dot(left, right, preferred_element_type=F32)


class Place:
    def __init__(self):
        dp, t = lax.axis_index("dp"), lax.axis_index("tensor")
        self.c, self.x = lax.rem(dp, 2), lax.rem(lax.div(dp, 2), RING)
        self.y, self.zhi = lax.div(t, 2), lax.rem(t, 2)
        self.z = self.zhi * 2 + lax.div(dp, 8)

    def at(self, x=None, y=None, z=None, c=None):
        x = self.x if x is None else x
        y = self.y if y is None else y
        z = self.z if z is None else z
        c = self.c if c is None else c
        return (lax.rem(z, 2) * 8 + x * 2 + c, y * 2 + lax.div(z, 2))

    def ring(self, axis):
        p = getattr(self, axis)
        ids = [self.at(**{axis: lax.rem(p + d, RING)}) for d in (1, 3, 2)]
        return (p, *ids)

    def partner(self):
        return self.at(c=1 - self.c)


class Links:
    def __init__(self, send, recv, local=None):
        self.send, self.recv, self.local = send, recv, local
        self.n = 0
        self.m = 0
        self.sent = []

    def push(self, src, dst, dev):
        copy = pltpu.make_async_remote_copy(
            src_ref=src, dst_ref=dst, send_sem=self.send.at[self.n],
            recv_sem=self.recv.at[self.n], device_id=dev, device_id_type=MESH,
        )
        self.n += 1
        copy.start()
        self.sent.append(copy)
        return copy

    def near(self, src, dst):
        copy = pltpu.make_async_copy(src, dst, self.local.at[self.m])
        self.m += 1
        copy.start()
        return copy

    def close(self):
        for copy in self.sent:
            copy.wait_send()


def greet(devs):
    barrier = pltpu.get_barrier_semaphore()
    for dev in devs:
        pl.semaphore_signal(barrier, inc=1, device_id=dev, device_id_type=MESH)
    pl.semaphore_wait(barrier, len(devs))


def around(p):
    return lax.rem(p + 3, RING), lax.rem(p + 1, RING), lax.rem(p + 2, RING)


def ring_gather(links, ring, slot, arrived=None, staged=False):
    p, right, left, _ = ring
    before, after, far = around(p)
    arrived = arrived or (lambda k, h: None)
    r0 = links.push(slot(p, 0), slot(p, 0), right)
    if staged:
        l0 = links.push(slot(p, 0), slot(p, 0), left)
        yield
    l1 = links.push(slot(p, 1), slot(p, 1), left)
    r1 = links.push(slot(p, 1), slot(p, 1), right)
    if not staged:
        l0 = links.push(slot(p, 0), slot(p, 0), left)
    yield
    r0.wait_recv()
    f0 = links.push(slot(before, 0), slot(before, 0), right)
    arrived(before, 0)
    l1.wait_recv()
    f1 = links.push(slot(after, 1), slot(after, 1), left)
    arrived(after, 1)
    yield
    r1.wait_recv()
    arrived(before, 1)
    l0.wait_recv()
    arrived(after, 0)
    f0.wait_recv()
    arrived(far, 0)
    f1.wait_recv()
    arrived(far, 1)


def ring_reduce(links, ring, part, buf, add, staged=False):
    p, right, left, _ = ring
    before, after, far = around(p)
    a = links.push(part(far, 0), buf[0], right)
    if staged:
        d = links.push(part(before, 0), buf[3], left)
        yield
    b = links.push(part(far, 1), buf[1], left)
    c = links.push(part(after, 1), buf[2], right)
    if not staged:
        d = links.push(part(before, 0), buf[3], left)
    yield
    a.wait_recv()
    add(buf[0], part(after, 0))
    f = links.push(buf[0], buf[4], right)
    b.wait_recv()
    add(buf[1], part(before, 1))
    g = links.push(buf[1], buf[5], left)
    yield
    for copy in (c, d, f, g):
        copy.wait_recv()


def drain(gen):
    for _ in gen:
        pass


def rows_of(q):
    return pl.ds(16 * q, 16)


def weight_gather(links, at, full):
    x, z, c = at.x, at.z, at.c
    ring_x, ring_z, mate = at.ring("x"), at.ring("z"), at.partner()
    a1 = ring_gather(links, ring_z, lambda k, h: full.at[:, k, x, c, rows_of(h)])
    b1 = ring_gather(links, ring_x, lambda k, h: full.at[:, z, k, c, rows_of(2 + h)])
    for i in range(3):
        next(a1, None)
        next(b1, None)
        if i < 2:
            yield

    crossed = []

    def cross(view):
        crossed.append(links.push(view, view, mate))

    slot_a = lambda k, h: full.at[:, :, k, c, rows_of(h)]
    slot_b = lambda k, h: full.at[:, k, :, c, rows_of(2 + h)]
    a2 = ring_gather(links, ring_x, slot_a, arrived=lambda k, h: cross(slot_a(k, h)))
    b2 = ring_gather(links, ring_z, slot_b, arrived=lambda k, h: cross(slot_b(k, h)))
    next(a2)
    next(b2)
    for h in range(2):
        cross(slot_a(x, h))
        cross(slot_b(z, h))
    yield
    for _ in range(2):
        next(a2, None)
        next(b2, None)
        yield
    for copy in crossed:
        copy.wait_recv()


def plus(*terms):
    total = terms[0].astype(F32)
    for t in terms[1:]:
        total = total + t.astype(F32)
    return total


def add_rows(dst, src):
    if len(dst.shape) == 3:
        for i in range(dst.shape[0]):
            dst[i] = plus(dst[i], src[i]).astype(BF)
        return

    def body(i, _):
        l, k = lax.div(i, RING), lax.rem(i, RING)
        dst[l, k] = plus(dst[l, k], src[l, k]).astype(BF)
        return 0

    lax.fori_loop(0, dst.shape[0] * RING, body, 0)


def weight_reduce(links, at, grads, total, bufs1, bufs2, outs):
    x, z, c = at.x, at.z, at.c
    ring_x, ring_z, mate = at.ring("x"), at.ring("z"), at.partner()
    arrays = grads.shape[0]
    swaps = [
        links.push(grads.at[:, k, :, 1 - c], total.at[:, k], mate) for k in range(RING)
    ]
    yield
    for k in range(RING):
        swaps[k].wait_recv()

        def body(i, _, k=k):
            l, j = lax.div(i, RING), lax.rem(i, RING)
            total[l, k, j] = plus(grads[l, k, j, c], total[l, k, j]).astype(BF)
            return 0

        lax.fori_loop(0, arrays * RING, body, 0)

    bufs = lambda ref, color: [ref.at[color, i] for i in range(6)]
    part_a = lambda k, h: total.at[:, :, k, rows_of(h)]
    part_b = lambda k, h: total.at[:, k, :, rows_of(2 + h)]
    a1 = ring_reduce(links, ring_x, part_a, bufs(bufs1, 0), add_rows)
    b1 = ring_reduce(links, ring_z, part_b, bufs(bufs1, 1), add_rows)
    for i in range(3):
        next(a1, None)
        next(b1, None)
        if i < 2:
            yield

    def close1(buf, own, h):
        one, two = (buf[3], buf[4]) if h == 0 else (buf[2], buf[5])

        def body(i, _):
            l, k = lax.div(i, RING), lax.rem(i, RING)
            own[l, k] = plus(own[l, k], one[l, k], two[l, k]).astype(BF)
            return 0

        lax.fori_loop(0, arrays * RING, body, 0)

    for h in range(2):
        close1(bufs(bufs1, 0), part_a(x, h), h)
        close1(bufs(bufs1, 1), part_b(z, h), h)
    part_a2 = lambda k, h: total.at[:, k, x, rows_of(h)]
    part_b2 = lambda k, h: total.at[:, z, k, rows_of(2 + h)]
    a2 = ring_reduce(links, ring_z, part_a2, bufs(bufs2, 0), add_rows)
    b2 = ring_reduce(links, ring_x, part_b2, bufs(bufs2, 1), add_rows)
    for i in range(3):
        next(a2, None)
        next(b2, None)
        if i < 2:
            yield
    for color, own in ((0, lambda h: part_a2(z, h)), (1, lambda h: part_b2(x, h))):
        buf = bufs(bufs2, color)
        for h in range(2):
            one, two = (buf[3], buf[4]) if h == 0 else (buf[2], buf[5])
            for l in range(arrays):
                outs[l][rows_of(2 * color + h)] = plus(own(h)[l], one[l], two[l])


def add_tokens(dst, src):
    for i in range(8):
        r = rows_of(i)
        dst[r] = plus(dst[r], src[r]).astype(BF)


def lanes_of(h):
    return pl.ds(512 * h, 512)


class TokenSum:
    def __init__(self, links, ring, part, land):
        self.part, self.land, self.p = part, [land.at[i] for i in range(6)], ring[0]
        self.steps = ring_reduce(
            links, ring, lambda k, h: part.at[k, :, lanes_of(h)], self.land, add_tokens, True
        )

    def produce(self, chunk):
        for h in range(2):

            def body(j, _, h=h):
                n = 2 * h + j
                value = chunk(n).astype(BF).reshape(RING, 128, 256)
                self.part[:, :, pl.ds(pl.multiple_of(n * 256, 256), 256)] = value
                return 0

            lax.fori_loop(0, 2, body, 0)
            next(self.steps)

    def rows(self, i):
        r, land = rows_of(i), self.land
        lo = plus(self.part[self.p, r, lanes_of(0)], land[3][r], land[4][r])
        hi = plus(self.part[self.p, r, lanes_of(1)], land[2][r], land[5][r])
        return jnp.concatenate([lo, hi], 1)


def quarter(n):
    return lax.div(n, 2), pl.ds(2 * lax.rem(n, 2), 2)


def inverse_rms(v):
    return lax.rsqrt(jnp.mean(v * v, -1, keepdims=True) + EPS)


def block_kernel(
    x_ref, gain1, wb, wc, wx, wo, taps_ref, gain2, cot_ref, wg, wu, wd,
    out_ref, gin_ref, n1_out, gb_out, gc_out, gx_out, conv_out, go_out, n2_out,
    gg_out, gu_out, gd_out,
    mix, ffn, h1, h2, cots, dmids, taps, bp, xp, cp, gext, conv, dext, ymix, dmix,
    mid, dmid, act, dgate, dup, part_mid, part_back, part_down, part_in, land,
    mix_g, mix_t, mix_b1, mix_b2, ffn_g, ffn_t, ffn_b1, ffn_b2, small, send, recv, local,
):
    at = Place()
    links = Links(send, recv, local)
    ring_y, ring_x, ring_z = at.ring("y"), at.ring("x"), at.ring("z")
    dp, t = lax.axis_index("dp"), lax.axis_index("tensor")
    n_dp = lax.axis_size("dp")
    p, zhi = at.y, at.zhi
    flip = t + 1 - 2 * zhi
    beside = (lax.rem(dp + n_dp + 2 * zhi - 1, n_dp), flip)
    own0 = [links.near(w, mix.at[i, at.z, at.x, at.c]) for i, w in enumerate((wb, wc, wx, wo))]
    own1 = [links.near(w, ffn.at[i, at.z, at.x, at.c]) for i, w in enumerate((wg, wu, wd))]
    for i in range(8):
        r = rows_of(i)
        v = x_ref[r]
        h1[p, r] = (v * inverse_rms(v) * gain1[...]).astype(BF)
    taps[zhi] = taps_ref[...]
    greet([*ring_y[1:4], *ring_x[1:4], *ring_z[1:4], at.partner(), beside])

    rows_half = lambda ref: lambda k, h: ref.at[k, pl.ds(64 * h, 64)]
    tok1 = ring_gather(links, ring_y, rows_half(h1))
    next(tok1)
    for copy in own0:
        copy.wait()
    mix_in = weight_gather(links, at, mix)
    next(mix_in)
    tap = links.push(taps_ref, taps.at[zhi], ring_z[3])
    for copy in own1:
        copy.wait()
    for i in range(8):
        r = rows_of(i)
        cots[p, r] = cot_ref[r].astype(BF)
    next(mix_in)
    next(tok1)
    next(mix_in)
    ffn_in = weight_gather(links, at, ffn)
    next(ffn_in)
    next(mix_in)
    next(mix_in)
    next(ffn_in)
    drain(tok1)
    drain(mix_in)

    def mixer(i):
        return jnp.concatenate(
            [mix[i, pl.ds(2 * s, 2)].reshape(1024, 128) for s in range(2)], 1
        )

    def mixer_rows(i, n):
        zz, xx = quarter(n)
        return jnp.concatenate(
            [mix[i, 2 * s + zz, xx].reshape(256, 128) for s in range(2)], 1
        )

    def ffn_half(i, s):
        return ffn[i, pl.ds(2 * s, 2)].reshape(1024, 576)

    def ffn_rows(i, s, n):
        zz, xx = quarter(n)
        return ffn[i, 2 * s + zz, xx].reshape(256, 576)

    def project(m, _):
        two = pl.ds(2 * m, 2)
        h = h1[two].reshape(256, 1024)
        b, x = dot(h, mixer(0)), dot(h, mixer(2))
        bp[two] = b.reshape(2, 128, 256)
        xp[two] = x.reshape(2, 128, 256)
        gext[two, pl.ds(8, 128)] = (b * x).reshape(2, 128, 256)
        return 0

    lax.fori_loop(0, 2, project, 0)
    tails = []
    for k in range(RING):
        to_dp = dp if k < 3 else lax.rem(dp + zhi, n_dp)
        tails.append(
            links.push(
                gext.at[k, pl.ds(128, 8)], gext.at[lax.rem(k + zhi, RING), pl.ds(0, 8)],
                (to_dp, flip),
            )
        )
    next(ffn_in)

    def project_c(m, _):
        two = pl.ds(2 * m, 2)
        cp[two] = dot(h1[two].reshape(256, 1024), mixer(1)).reshape(2, 128, 256)
        return 0

    lax.fori_loop(0, 2, project_c, 0)
    tap.wait_recv()
    for copy in tails:
        copy.wait_recv()
    row = lax.broadcasted_iota(jnp.int32, (128, 256), 0)
    tap_rows = jnp.concatenate([taps[0], taps[1]], 1)
    t0, t1, t2 = tap_rows[0:1], tap_rows[1:2], tap_rows[2:3]

    def keeps(r):
        begins = (r == 0) | (lax.rem(r * 128 + SEQ - OFFSET, SEQ) == 0)
        return jnp.where(begins | (r == n_dp * 8), 0.0, 1.0)

    def shifted(k):
        keep = keeps(dp * 8 + 2 * k + zhi)
        two, one = gext[k, pl.ds(6, 128)], gext[k, pl.ds(7, 128)]
        return jnp.where(row < 2, two * keep, two), jnp.where(row < 1, one * keep, one)

    def mixing(k, _):
        two, one = shifted(k)
        v = t0 * two + t1 * one + t2 * gext[k, pl.ds(8, 128)]
        conv[k] = v
        ymix[k] = (cp[k] * v).astype(BF)
        return 0

    lax.fori_loop(0, RING, mixing, 0)
    sum_mid = TokenSum(links, ring_y, part_mid, land.at[0])
    sum_mid.produce(lambda n: ndot(ymix[...].reshape(512, 256), mixer_rows(3, n)))
    next(ffn_in)
    next(sum_mid.steps)
    drain(sum_mid.steps)
    tok2 = ring_gather(links, ring_y, rows_half(h2), staged=True)
    for i in range(8):
        r = rows_of(i)
        v = x_ref[r] + sum_mid.rows(i)
        mid[r] = v
        h2[p, r] = (v * inverse_rms(v) * gain2[...]).astype(BF)
        if i % 4 == 3:
            next(tok2)
    tok_c = ring_gather(links, ring_y, rows_half(cots))
    next(tok_c)
    next(tok2)
    next(ffn_in)
    next(tok_c)
    drain(tok2)
    drain(tok_c)
    drain(ffn_in)

    def feed(i, _):
        s, m = lax.div(i, 2), lax.rem(i, 2)
        two = pl.ds(2 * m, 2)
        h = h2[two].reshape(256, 1024)
        gate, up = dot(h, ffn_half(0, s)), dot(h, ffn_half(1, s))
        dact = dot(cots[two].reshape(256, 1024), ffn_half(2, s))
        sig = jax.nn.sigmoid(gate)
        silu = gate * sig
        r = pl.ds(pl.multiple_of(m * 256, 256), 256)
        act[s, r] = (silu * up).astype(BF)
        dgate[s, r] = (dact * up * sig * (1.0 + gate * (1.0 - sig))).astype(BF)
        dup[s, r] = (dact * silu).astype(BF)
        return 0

    lax.fori_loop(0, 4, feed, 0)
    sum_back = TokenSum(links, ring_y, part_back, land.at[1])

    def back_chunk(n):
        v = ndot(dgate[0], ffn_rows(0, 0, n)) + ndot(dup[0], ffn_rows(1, 0, n))
        return v + ndot(dgate[1], ffn_rows(0, 1, n)) + ndot(dup[1], ffn_rows(1, 1, n))

    sum_back.produce(back_chunk)

    def ffn_grads(s, pairs):
        def body(n, _):
            zz, xx = quarter(n)
            cols = pl.ds(pl.multiple_of(n * 256, 256), 256)
            for i, tokens, right in pairs:
                left = tokens[:, :, cols].reshape(512, 256)
                g = tdot(left, right[s]).astype(BF)
                ffn_g[i, 2 * s + zz, xx] = g.reshape(2, 2, 64, 576)
            return 0

        lax.fori_loop(0, 4, body, 0)

    ffn_grads(0, ((0, h2, dgate), (1, h2, dup)))
    next(sum_back.steps)
    ffn_grads(1, ((0, h2, dgate), (1, h2, dup)))
    drain(sum_back.steps)
    tok3 = ring_gather(links, ring_y, rows_half(dmids), staged=True)
    norm2 = jnp.zeros((8, 1024), F32)
    for i in range(8):
        r = rows_of(i)
        dh = sum_back.rows(i)
        v = mid[r]
        r2 = inverse_rms(v)
        n2 = v * r2
        w = dh * n2
        norm2 = norm2 + w[:8] + w[8:]
        dn = dh * gain2[...]
        dm = cot_ref[r] + r2 * (dn - n2 * jnp.mean(dn * n2, -1, keepdims=True))
        dmid[r] = dm
        dmids[p, r] = dm.astype(BF)
        if i % 4 == 3:
            next(tok3)
    ffn_grads(0, ((2, cots, act),))
    next(tok3)
    ffn_grads(1, ((2, cots, act),))
    ffn_out = weight_reduce(links, at, ffn_g, ffn_t, ffn_b1, ffn_b2, (gg_out, gu_out, gd_out))
    next(ffn_out)
    sum_down = TokenSum(links, ring_y, part_down, land.at[2])
    sum_down.produce(
        lambda n: ndot(act[0], ffn_rows(2, 0, n)) + ndot(act[1], ffn_rows(2, 1, n))
    )
    drain(tok3)
    next(ffn_out)

    def spread(m, _):
        two = pl.ds(2 * m, 2)
        dy = dot(dmids[two].reshape(256, 1024), mixer(3)).reshape(2, 128, 256)
        dext[two, pl.ds(0, 128)] = dy * cp[two]
        dc = (dy * conv[two]).astype(BF).reshape(256, 256)
        dmix[pl.ds(pl.multiple_of(m * 256, 256), 256), pl.ds(256, 256)] = dc
        return 0

    lax.fori_loop(0, 2, spread, 0)
    heads = []
    for k in range(RING):
        to_dp = dp if k > 0 else lax.rem(dp + n_dp + zhi - 1, n_dp)
        heads.append(
            links.push(
                dext.at[k, pl.ds(0, 8)], dext.at[lax.rem(k + 3 + zhi, RING), pl.ds(128, 8)],
                (to_dp, flip),
            )
        )
    next(sum_down.steps)

    def mix_grads(i, tokens, right):
        def body(n, _):
            zz, xx = quarter(n)
            cols = pl.ds(pl.multiple_of(n * 256, 256), 256)
            g = tdot(tokens[:, :, cols].reshape(512, 256), right()).astype(BF)
            for s in range(2):
                mix_g[i, 2 * s + zz, xx] = g[:, 128 * s : 128 * s + 128].reshape(2, 2, 64, 128)
            return 0

        lax.fori_loop(0, 4, body, 0)

    mix_grads(3, dmids, lambda: ymix[...].reshape(512, 256))
    for copy in heads:
        copy.wait_recv()

    def unmix(k, carry):
        keep = keeps(dp * 8 + 2 * k + zhi + 1)
        d = dext[k, pl.ds(0, 128)]
        one, two = dext[k, pl.ds(1, 128)], dext[k, pl.ds(2, 128)]
        one = jnp.where(row >= 127, one * keep, one)
        two = jnp.where(row >= 126, two * keep, two)
        dg = t2 * d + t1 * one + t0 * two
        r = pl.ds(pl.multiple_of(k * 128, 128), 128)
        dmix[r, pl.ds(0, 256)] = (dg * xp[k]).astype(BF)
        dmix[r, pl.ds(512, 256)] = (dg * bp[k]).astype(BF)
        g2, g1 = shifted(k)
        terms = (g2, g1, gext[k, pl.ds(8, 128)])
        return tuple(c + jnp.sum(d * v, 0, keepdims=True) for c, v in zip(carry, terms))

    zero = jnp.zeros((1, 256), F32)
    conv_sums = lax.fori_loop(0, RING, unmix, (zero, zero, zero))
    sum_in = TokenSum(links, ring_y, part_in, land.at[3])

    def in_chunk(n):
        w = jnp.concatenate([mixer_rows(i, n) for i in range(3)], 1)
        return ndot(dmix[...], w)

    sum_in.produce(in_chunk)
    next(ffn_out)
    drain(sum_down.steps)
    for i in range(8):
        r = rows_of(i)
        out_ref[r] = mid[r] + sum_down.rows(i)
    for i in range(3):
        mix_grads(i, h1, lambda i=i: dmix[:, 256 * i : 256 * i + 256])
        if i == 1:
            next(sum_in.steps)
    mix_out = weight_reduce(links, at, mix_g, mix_t, mix_b1, mix_b2, (gb_out, gc_out, gx_out, go_out))
    next(mix_out)
    next(ffn_out)
    next(mix_out)
    drain(sum_in.steps)
    norm1 = jnp.zeros((8, 1024), F32)
    for i in range(8):
        r = rows_of(i)
        dh = sum_in.rows(i)
        v = x_ref[r]
        r1 = inverse_rms(v)
        n1 = v * r1
        w = dh * n1
        norm1 = norm1 + w[:8] + w[8:]
        dn = dh * gain1[...]
        gin_ref[r] = dmid[r] + r1 * (dn - n1 * jnp.mean(dn * n1, -1, keepdims=True))
    small[0, p] = jnp.zeros((8, 1024), F32)
    small[0, p, 0:1] = jnp.sum(norm1, 0, keepdims=True)
    small[0, p, 1:2] = jnp.sum(norm2, 0, keepdims=True)
    for i in range(3):
        small[0, p, pl.ds(2 + i, 1), pl.ds(pl.multiple_of(p * 256, 256), 256)] = conv_sums[i]
    for s, ring in enumerate((ring_y, ring_x, ring_z)):
        pos = ring[0]
        copies = [links.push(small.at[s, pos], small.at[s, pos], dev) for dev in ring[1:4]]
        next(ffn_out, None)
        next(mix_out, None)
        for copy in copies:
            copy.wait_recv()
        value = (small[s, 0] + small[s, 1]) + (small[s, 2] + small[s, 3])
        if s < 2:
            small[s + 1, (ring_x, ring_z)[s][0]] = value
        else:
            small[3, at.c] = value
    copy = links.push(small.at[3, at.c], small.at[3, at.c], at.partner())
    next(mix_out, None)
    copy.wait_recv()
    value = small[3, 0] + small[3, 1]
    n1_out[...] = value[0:1]
    n2_out[...] = value[1:2]
    small[3, 2] = value
    conv_out[...] = small[3, 2, pl.ds(2, 3), pl.ds(pl.multiple_of(t * 128, 128), 128)]
    drain(ffn_out)
    drain(mix_out)
    links.close()


VM = pl.BlockSpec(memory_space=pltpu.VMEM)
ANY = pl.BlockSpec(memory_space=pl.ANY)


def per_device(
    block_in, norm1_gain, w_b, w_c, w_x, conv_w, w_out, norm2_gain, w_gate, w_up, w_down, out_cot
):
    f = lambda *shape: jax.ShapeDtypeStruct(shape, F32)
    bf = lambda *shape: pltpu.VMEM(shape, BF)
    fl = lambda *shape: pltpu.VMEM(shape, F32)
    tokens = bf(RING, 128, 1024)
    plane = fl(RING, 128, 256)
    sems = pltpu.SemaphoreType.DMA
    outs = pl.pallas_call(
        block_kernel,
        out_shape=[
            f(128, 1024), f(128, 1024), f(1, 1024), f(64, 128), f(64, 128), f(64, 128),
            f(3, 128), f(64, 128), f(1, 1024), f(64, 576), f(64, 576), f(64, 576),
        ],
        in_specs=[VM, VM, ANY, ANY, ANY, ANY, VM, VM, VM, ANY, ANY, ANY],
        out_specs=[VM] * 12,
        scratch_shapes=[
            bf(4, 4, 4, 2, 64, 128), bf(3, 4, 4, 2, 64, 576),
            tokens, tokens, tokens, tokens,
            fl(2, 3, 128), plane, plane, plane, fl(RING, 136, 256), plane, fl(RING, 136, 256),
            bf(RING, 128, 256), bf(512, 768), fl(128, 1024), fl(128, 1024),
            bf(2, 512, 576), bf(2, 512, 576), bf(2, 512, 576),
            tokens, tokens, tokens, tokens, bf(4, 6, 128, 512),
            bf(4, 4, 4, 2, 64, 128), bf(4, 4, 4, 64, 128), bf(2, 6, 4, 4, 16, 128),
            bf(2, 6, 4, 16, 128),
            bf(3, 4, 4, 2, 64, 576), bf(3, 4, 4, 64, 576), bf(2, 6, 3, 4, 16, 576),
            bf(2, 6, 3, 16, 576),
            fl(4, RING, 8, 1024), sems((256,)), sems((256,)), sems((8,)),
        ],
        compiler_params=pltpu.CompilerParams(
            collective_id=0, has_side_effects=True, vmem_limit_bytes=VMEM_LIMIT
        ),
    )(
        block_in, norm1_gain[None, :], w_b, w_c, w_x, w_out.T, conv_w, norm2_gain[None, :],
        out_cot, w_gate, w_up, w_down.T,
    )
    out, gin, n1, gb, gc, gx, gconv, go, n2, gg, gu, gd = outs
    return (out, gin, n1[0], gb, gc, gx, gconv, go.T, n2[0], gg, gu, gd.T)


def solution(mesh):
    tok, mat, tam = P(("dp", "tensor"), None), P("dp", "tensor"), P("tensor", "dp")
    taps = P(None, "tensor")
    return jax.shard_map(
        per_device,
        mesh=mesh,
        in_specs=(tok, P(), mat, mat, mat, taps, tam, P(), mat, mat, tam, tok),
        out_specs=(tok, tok, P(), mat, mat, mat, taps, tam, P(), mat, mat, tam),
        check_vma=False,
    )
```
